128 devices in a mesh: row: 8 (over y, core), col: 16 (over z, x).
Axes of the slice: x: 4, y: 4, z: 4, core: 2. Of those that a mesh axis runs over, the one named last changes fastest.
Arguments:
- rhs_scen: bfloat16 [1024, 131072], P(('row', 'col')), may hold values from -6 to 6
- factor_panels: bfloat16 [131072, 8192], P(('row', 'col')), as said below
Outputs:
- current: float32 [131072, 1024], P(('row', 'col'))
The draws below stay inside these ranges and needn't reach their ends.
Inputs may be any that keep to these rules, and one draw needn't show every extreme that they name: `factor_panels`: in the rows of block b (b < 4, blocks of 2048 rows), every entry in the columns of later blocks is zero, and so is every entry above the diagonal of block b's own columns.
All inputs are finite; a program needn't handle non-finite values.
Results may differ from the reference program's by a relative error of at most 0.0023.
Values may be sent and summed in bfloat16 or wider, within the bound.
A program may use at most 128 MiB of HBM per device.

```python
import math
import jax
import jax.numpy as jnp

NB = 2048
STEPS = 4
NORD = 131072
SCEN = 1024


def draw_factor_panels(key, part):
    row_ids = jnp.arange(NORD, dtype=jnp.int32)[:, None]
    col_ids = jnp.arange(STEPS * NB, dtype=jnp.int32)[None, :]
    base = jax.random.truncated_normal(key, -4.0, 4.0, (NORD, STEPS * NB), jnp.float32)
    scaled = base * (0.5 / math.sqrt(NB))
    row_block = row_ids // NB
    col_block = col_ids // NB
    inner_row = row_ids % NB
    inner_col = col_ids % NB
    diag_value = 1.0 + 0.3 * jnp.tanh(base)
    within = jnp.where(inner_row == inner_col, diag_value, jnp.where(inner_row > inner_col, 1.2 * scaled, 0.0))
    return jnp.where(row_block == col_block, within, jnp.where(row_block > col_block, scaled, 0.0)).astype(jnp.bfloat16)


def levels(own_key, extent, pieces, smallest, top_value):
    def one(position, parts):
        heights = jax.random.uniform(jax.random.fold_in(jax.random.fold_in(own_key, 6), position), (parts,), jnp.float32, smallest / len(pieces), top_value / len(pieces))
        return jnp.repeat(jnp.exp(heights), extent[position] // parts).reshape((-1,) + (1,) * (len(extent) - position - 1))

    factor_of = one(*pieces[0])
    for cut in pieces[1:]:
        factor_of = factor_of * one(*cut)
    return factor_of


def noise(stream_key, extent, spread, most, split=(), held_as=jnp.bfloat16):
    factor_of = levels(stream_key, extent, split, -0.22, 0.18) if split else 1.0
    array = jax.random.normal(stream_key, extent, jnp.float32) * spread * factor_of
    return jnp.minimum(jnp.maximum(array, -most), most).astype(held_as)


def setup_inputs(seed: int = 0) -> dict:
    key_list = jax.random.split(jax.random.key(seed), 3)
    return {
        "rhs_scen": noise(key_list[0], (SCEN, NORD), 1.0, 6.0, ((0, 128),)),
        "factor_panels": draw_factor_panels(jax.random.fold_in(key_list[2], 71), 0),
    }


def reference(rhs_scen, factor_panels):
    current = jnp.transpose(rhs_scen).astype(jnp.float32)
    for block_step in range(STEPS):
        lower = block_step * NB
        outgoing = current[lower:lower + NB].astype(jnp.bfloat16)
        product = jnp.dot(factor_panels[:, lower:lower + NB], outgoing, preferred_element_type=jnp.float32)
        updated = current - product
        current = updated.at[lower:lower + NB].set(product[lower:lower + NB])
    return current
```

```python
import jax
import jax.numpy as jnp
from jax import lax
from jax.experimental import pallas as pl
from jax.experimental.pallas import tpu as pltpu
from jax.sharding import PartitionSpec as P

NB = 2048
STEPS = 4
ROWS = 1024
SCEN = 1024
T = 256
MESH = pl.DeviceIdType.MESH
ALL = slice(None)

COLOURS = (
    ("xzy", (0, ALL, pl.ds(0, 640)), (0, ALL, pl.ds(0, 384)), (0, ALL, pl.ds(384, 256))),
    ("yxz", (1, ALL, pl.ds(0, 640)), (1, ALL, pl.ds(0, 256)), (1, ALL, pl.ds(256, 384))),
    ("zyx", (ALL, ALL, pl.ds(640, 384)), (0, ALL, pl.ds(640, 384)), (1, ALL, pl.ds(640, 384))),
)
AXES = "yzx"


def kernel(rhs, panels, out, xs, acc, fac, rt, staged, own_sem, fac_sem, send_sem, recv_sem, xsend_sem, xrecv_sem,
           rt_send, rt_recv, sc_send):
    row, col = lax.axis_index("row"), lax.axis_index("col")
    me = row * 16 + col
    core = row % 2
    at = {"y": row // 2, "z": col // 4, "x": col % 4}
    my_block = me // 2

    def device(place, on_core):
        return (place["y"] * 2 + on_core, place["z"] * 4 + place["x"])

    def moved(axis, by):
        return {**at, axis: (at[axis] + by) % 4}

    def rows_to(dst):
        return rhs.at[:, pl.ds(pl.multiple_of(dst * ROWS, ROWS), ROWS)]

    def rt_copy(dst):
        return pltpu.make_async_remote_copy(
            src_ref=rows_to(dst), dst_ref=rt.at[core, at["y"], at["z"], at["x"]], send_sem=rt_send, recv_sem=rt_recv,
            device_id=(dst // 16, dst % 16), device_id_type=MESH)

    def rt_batch(first, last):
        def one(j, carry):
            dst = (me + j) % 128

            @pl.when((dst < 2) | (dst > 7))
            def _():
                rt_copy(dst).start()
            return carry
        lax.fori_loop(first, last, one, 0)

    def rt_wait():
        pltpu.make_async_copy(rt, rt, rt_recv).wait()

    def load_factor(k):
        cols = pl.ds(k * NB, NB)
        return pltpu.make_async_copy(panels.at[:, cols], fac.at[:, cols], fac_sem.at[k])

    def block_of(k, colour, fixed, part):
        return xs.at[(k, core) + tuple(fixed.get(a, ALL) for a in AXES) + part]

    def gather(k):
        started = []

        def ring(colour, phase, lane, by, centre, part):
            order = COLOURS[colour][0]
            axis, later = order[phase], order[phase + 1:]
            fixed = {a: at[a] for a in later}
            fixed[axis] = (at[axis] + centre) % 4
            block = block_of(k, colour, fixed, part)
            return pltpu.make_async_remote_copy(
                src_ref=block, dst_ref=block, send_sem=send_sem.at[phase, colour, lane],
                recv_sem=recv_sem.at[k, phase, colour, lane], device_id=device(moved(axis, by), core), device_id_type=MESH)

        def exchange(colour, step, centre):
            order, whole = COLOURS[colour][:2]
            axis = order[2]
            block = block_of(k, colour, {axis: (at[axis] + centre) % 4}, whole)
            copy = pltpu.make_async_remote_copy(
                src_ref=block, dst_ref=block, send_sem=xsend_sem.at[colour, step], recv_sem=xrecv_sem.at[k, colour, step],
                device_id=device(at, 1 - core), device_id_type=MESH)
            copy.start()
            started.append(copy)
            return copy

        swaps = []
        for phase in range(3):
            first = []
            for colour in range(3):
                whole = COLOURS[colour][1]
                first.append((ring(colour, phase, 0, 1, 0, whole), ring(colour, phase, 1, -1, 0, whole)))
            for pair in first:
                for copy in pair:
                    copy.start()
                    started.append(copy)
            if phase == 2:
                for colour in range(3):
                    swaps.append(exchange(colour, 0, 0))
            second = []
            for colour in range(3):
                _, _, low, high = COLOURS[colour]
                first[colour][0].wait_recv()
                onward = ring(colour, phase, 2, 1, -1, low)
                onward.start()
                first[colour][1].wait_recv()
                back = ring(colour, phase, 3, -1, 1, high)
                back.start()
                second += [onward, back]
            started += second
            if phase == 2:
                for colour in range(3):
                    swaps += [exchange(colour, 1, -1), exchange(colour, 2, 1)]
            for copy in second:
                copy.wait_recv()
        for colour in range(3):
            swaps.append(exchange(colour, 3, 2))
        for copy in swaps:
            copy.wait_recv()
        for copy in started:
            copy.wait_send()

    def product(k, m, n):
        rows = pl.ds(pl.multiple_of(m * T, T), T)
        cols = pl.ds(pl.multiple_of(n * T, T), T)
        left = fac[rows, pl.ds(pl.multiple_of(k * NB, NB), NB)]
        right = xs[k, :, :, :, :, :, :, cols].reshape(NB, T)
        return jnp.dot(left, right, preferred_element_type=jnp.float32)

    def turned(m, n):
        cols = pl.ds(pl.multiple_of(m * T, T), T)
        held = rt[n // 2, pl.ds((n % 2) * 2, 2), :, :, :, cols].reshape(T, T)
        eye = (lax.broadcasted_iota(jnp.int32, (T, T), 0) == lax.broadcasted_iota(jnp.int32, (T, T), 1))
        return lax.dot_general(eye.astype(jnp.bfloat16), held, (((1,), (1,)), ((), ())), preferred_element_type=jnp.float32)

    def tile(m, n):
        return pl.ds(pl.multiple_of(m * T, T), T), pl.ds(pl.multiple_of(n * T, T), T)

    def multiply_first():
        def one(i, carry):
            m, n = i % 4, i // 4
            rows, _ = tile(m, n)
            total = jnp.zeros((T, T), jnp.float32)
            for half in range(2):
                right = xs[0, n // 2, pl.ds((n % 2) * 2, 2), :, :, half].reshape(T, 1024)
                left = fac[rows, half * 1024:(half + 1) * 1024]
                total = total + lax.dot_general(left, right, (((1,), (1,)), ((), ())), preferred_element_type=jnp.float32)
            acc[tile(m, n)] = total
            return carry
        lax.fori_loop(0, 16, one, 0)

    def multiply(k):
        def one(i, carry):
            m, n = i % 4, i // 4
            kept = jnp.where(my_block == k, 0.0, acc[tile(m, n)])
            acc[tile(m, n)] = kept + product(k, m, n)
            return carry
        lax.fori_loop(0, 16, one, 0)

    def scatter_copies(k, m, i, go):
        z, x = i // 4, i % 4
        parity = me % 2
        src, dst = staged.at[m, z, x], xs.at[k, parity, m, z, x]
        here = (m == at["y"]) & (z == at["z"]) & (x == at["x"]) & (parity == core)

        @pl.when(here)
        def _():
            pltpu.make_async_copy(src, dst, own_sem.at[k]).start()

        @pl.when(jnp.logical_not(here))
        def _():
            pltpu.make_async_remote_copy(
                src_ref=src, dst_ref=dst, send_sem=sc_send, recv_sem=own_sem.at[k],
                device_id=(m * 2 + parity, i), device_id_type=MESH).start()

    def solve(k):
        rt_wait()

        def row_tile(m, carry):
            def col_tile(n, inner):
                solved = turned(m, n) - acc[tile(m, n)]
                staged[m, :, :, :, :, tile(m, n)[1]] = solved.astype(jnp.bfloat16).reshape(4, 4, 2, 8, T)
                return inner
            lax.fori_loop(0, 4, col_tile, 0)

            def send(i, inner):
                scatter_copies(k, m, i, True)
                return inner
            lax.fori_loop(0, 16, send, 0)
            return carry
        lax.fori_loop(0, 4, row_tile, 0)

    loads = [load_factor(k) for k in range(STEPS)]
    for load in loads:
        load.start()
    for half in range(2):
        pltpu.make_async_copy(
            rhs.at[:, half * 1024:(half + 1) * 1024], xs.at[0, core, at["y"], at["z"], at["x"], half], own_sem.at[0]).start()
    mine = pltpu.make_async_copy(rows_to(me), rt.at[core, at["y"], at["z"], at["x"]], rt_recv)
    mine.start()

    for owner in range(2, 8):
        @pl.when(me != owner)
        def _():
            rt_copy(jnp.int32(owner)).start()

    def own_piece(k):
        piece = xs.at[k, core, at["y"], at["z"], at["x"]]
        pltpu.make_async_copy(piece, piece, own_sem.at[k]).wait()

    own_piece(0)
    gather(0)
    for load in loads:
        load.wait()
    rt_batch(1, 44)
    multiply_first()

    def step(k, carry):
        @pl.when(my_block == k)
        def _():
            solve(k)
        own_piece(k)
        gather(k)

        @pl.when(k < STEPS - 1)
        def _():
            rt_batch(k * 43 + 1, jnp.minimum(k * 43 + 44, 128))
            multiply(k)
        return carry

    lax.fori_loop(1, STEPS, step, 0)

    is_owner = me < 2 * STEPS

    @pl.when((me < 2) | (me > 7))
    def _():
        rt_wait()

    for c in range(2):
        for pair in range(2):
            n = c * 2 + pair

            def last(m, carry):
                rows, _ = tile(m, n)
                kept = jnp.where(my_block == STEPS - 1, 0.0, acc[tile(m, n)])
                total = kept + product(STEPS - 1, m, n)
                value = jnp.where(is_owner, total, turned(m, n) - total)
                for y in range(2):
                    out[rows, ((pair * 2 + y) * 2 + c) * 128:((pair * 2 + y) * 2 + c + 1) * 128] = value[:, y * 128:(y + 1) * 128]
                return carry
            lax.fori_loop(0, 4, last, 0)

    pltpu.make_async_copy(rt.at[0], rt.at[0], rt_send).wait()
    pltpu.make_async_copy(rt.at[1, 0:3], rt.at[1, 0:3], rt_send).wait()
    pltpu.make_async_copy(rt.at[1, 3, 0:3], rt.at[1, 3, 0:3], rt_send).wait()
    pltpu.make_async_copy(rt.at[1, 3, 3, 0:3], rt.at[1, 3, 3, 0:3], rt_send).wait()

    @pl.when((me >= 2) & (me < 8))
    def _():
        @pl.when(me % 2 == 1)
        def _():
            pltpu.make_async_copy(staged, staged, sc_send).wait()

        @pl.when(me % 2 == 0)
        def _():
            pltpu.make_async_copy(staged.at[0:3], staged.at[0:3], sc_send).wait()
            pltpu.make_async_copy(staged.at[3, 0:3], staged.at[3, 0:3], sc_send).wait()
            pltpu.make_async_copy(staged.at[3, 3, 0:3], staged.at[3, 3, 0:3], sc_send).wait()


def on_device(rhs_scen, factor_panels):
    dma = pltpu.SemaphoreType.DMA
    return pl.pallas_call(
        kernel,
        out_shape=jax.ShapeDtypeStruct((ROWS, SCEN), jnp.float32),
        in_specs=[pl.BlockSpec(memory_space=pl.ANY)] * 2,
        out_specs=pl.BlockSpec(memory_space=pltpu.VMEM),
        scratch_shapes=[
            pltpu.VMEM((STEPS, 2, 4, 4, 4, 2, 8, 1024), jnp.bfloat16),
            pltpu.VMEM((ROWS, SCEN), jnp.float32),
            pltpu.VMEM((ROWS, STEPS * NB), jnp.bfloat16),
            pltpu.VMEM((2, 4, 4, 4, 8, ROWS), jnp.bfloat16),
            pltpu.VMEM((4, 4, 4, 2, 8, SCEN), jnp.bfloat16),
            dma((STEPS,)), dma((STEPS,)), dma((3, 3, 4)), dma((STEPS, 3, 3, 4)), dma((3, 4)), dma((STEPS, 3, 4)),
            dma, dma, dma,
        ],
        compiler_params=pltpu.CompilerParams(has_side_effects=True, vmem_limit_bytes=60 * 1024 * 1024),
        name="substitute",
    )(rhs_scen, factor_panels)


def solution(mesh):
    placed = (P(("row", "col"), None), P(("row", "col"), None))
    return jax.shard_map(
        on_device, mesh=mesh, in_specs=placed, out_specs=P(("row", "col"), None), check_vma=False
    )
```

```python
import jax
import jax.numpy as jnp
from jax import lax
from jax.experimental import pallas as pl
from jax.experimental.pallas import tpu as pltpu
from jax.sharding import PartitionSpec as P

NB = 2048
STEPS = 4
ROWS = 1024
SCEN = 1024
T = 256
MESH = pl.DeviceIdType.MESH
ALL = slice(None)

COLOURS = (
    ("xzy", (0, ALL, pl.ds(0, 640)), (0, ALL, pl.ds(0, 384)), (0, ALL, pl.ds(384, 256))),
    ("yxz", (1, ALL, pl.ds(0, 640)), (1, ALL, pl.ds(0, 256)), (1, ALL, pl.ds(256, 384))),
    ("zyx", (ALL, ALL, pl.ds(640, 384)), (0, ALL, pl.ds(640, 384)), (1, ALL, pl.ds(640, 384))),
)
AXES = "yzx"

WAYS = [(axis, by) for axis in "xyz" for by in (1, -1)]


def plan_relays():
    relays = {way: [[] for _ in range(4)] for way in WAYS}
    load = dict.fromkeys(WAYS, 0)
    for far in (1, 2, 3):
        for m in range(4):
            for dz in range(4):
                for dx in range(4):
                    offset = {"x": dx, "y": m, "z": dz}
                    moving = [a for a in "xyz" if offset[a]]
                    hops = sum(min(v, 4 - v) for v in offset.values())
                    if len(moving) != far or hops == 1:
                        continue
                    ways = [w for w in WAYS if offset[w[0]] == 2 or offset[w[0]] == w[1] % 4]
                    way = min(ways, key=lambda w: (load[w] + len(relays[w][m]), WAYS.index(w)))
                    load[way] += 1
                    relays[way][m].append((dz, dx))
    return relays


RELAYS = plan_relays()
MOST = max(len(part) for parts in RELAYS.values() for part in parts)


def kernel(rhs, panels, out, xs, acc, fac, rt, staged, passing, own_sem, fac_sem, send_sem, recv_sem, xsend_sem, xrecv_sem,
           rt_send, rt_recv, sc_send, pass_recv, pass_send):
    row, col = lax.axis_index("row"), lax.axis_index("col")
    me = row * 16 + col
    core = row % 2
    at = {"y": row // 2, "z": col // 4, "x": col % 4}
    my_block = me // 2

    def device(place, on_core):
        return (place["y"] * 2 + on_core, place["z"] * 4 + place["x"])

    def moved(axis, by):
        return {**at, axis: (at[axis] + by) % 4}

    def rows_to(dst):
        return rhs.at[:, pl.ds(pl.multiple_of(dst * ROWS, ROWS), ROWS)]

    def rt_copy(dst):
        return pltpu.make_async_remote_copy(
            src_ref=rows_to(dst), dst_ref=rt.at[core, at["y"], at["z"], at["x"]], send_sem=rt_send, recv_sem=rt_recv,
            device_id=(dst // 16, dst % 16), device_id_type=MESH)

    def rt_batch(first, last):
        def one(j, carry):
            dst = (me + j) % 128

            @pl.when((dst < 2) | (dst > 7))
            def _():
                rt_copy(dst).start()
            return carry
        lax.fori_loop(first, last, one, 0)

    def rt_wait():
        pltpu.make_async_copy(rt, rt, rt_recv).wait()

    def load_factor(k):
        cols = pl.ds(k * NB, NB)
        return pltpu.make_async_copy(panels.at[:, cols], fac.at[:, cols], fac_sem.at[k])

    def block_of(k, colour, fixed, part):
        return xs.at[(k, core) + tuple(fixed.get(a, ALL) for a in AXES) + part]

    def gather(k):
        started = []

        def ring(colour, phase, group, lane, by, centre, part):
            order = COLOURS[colour][0]
            axis, later = order[phase], order[phase + 1:]
            fixed = {a: at[a] for a in later}
            fixed[axis] = (at[axis] + centre) % 4
            slot = phase
            if phase == 2:
                fixed[order[1]] = (at[order[1]] + group) % 4
                slot = 2 + group % 4
            block = block_of(k, colour, fixed, part)
            copy = pltpu.make_async_remote_copy(
                src_ref=block, dst_ref=block, send_sem=send_sem.at[k, slot, colour, lane],
                recv_sem=recv_sem.at[k, slot, colour, lane], device_id=device(moved(axis, by), core), device_id_type=MESH)
            copy.start()
            started.append(copy)
            return copy

        def outward(colour, phase, group=0):
            whole = COLOURS[colour][1]
            return ring(colour, phase, group, 0, 1, 0, whole), ring(colour, phase, group, 1, -1, 0, whole)

        def onward(colour, phase, group=0):
            return ring(colour, phase, group, 2, 1, -1, COLOURS[colour][2])

        def back(colour, phase, group=0):
            return ring(colour, phase, group, 3, -1, 1, COLOURS[colour][3])

        def exchange(colour, step, centre):
            order, whole = COLOURS[colour][:2]
            axis = order[2]
            block = block_of(k, colour, {axis: (at[axis] + centre) % 4}, whole)
            copy = pltpu.make_async_remote_copy(
                src_ref=block, dst_ref=block, send_sem=xsend_sem.at[k, colour, step], recv_sem=xrecv_sem.at[k, colour, step],
                device_id=device(at, 1 - core), device_id_type=MESH)
            copy.start()
            started.append(copy)
            return copy

        three = range(3)
        first = [outward(c, 0) for c in three]
        far = []
        for c in three:
            first[c][0].wait_recv()
            one = onward(c, 0)
            first[c][1].wait_recv()
            far.append((one, back(c, 0)))
        second = []
        for c in three:
            far[c][0].wait_recv()
            far[c][1].wait_recv()
            second.append(outward(c, 1))
        last = {(c, 0): outward(c, 2, 0) for c in three}
        far = []
        for c in three:
            second[c][0].wait_recv()
            one = onward(c, 1)
            second[c][1].wait_recv()
            far.append((one, back(c, 1)))
        for group in (-1, 1):
            for c in three:
                last[c, group] = outward(c, 2, group)
        ends = []
        for c in three:
            last[c, 0][0].wait_recv()
            ends.append(onward(c, 2, 0))
            last[c, 0][1].wait_recv()
            ends.append(back(c, 2, 0))
        for c in three:
            far[c][0].wait_recv()
            far[c][1].wait_recv()
            last[c, 2] = outward(c, 2, 2)
        swaps = [exchange(c, 0, 0) for c in three]
        for group in (-1, 1, 2):
            for c in three:
                last[c, group][0].wait_recv()
                ends.append(onward(c, 2, group))
                last[c, group][1].wait_recv()
                ends.append(back(c, 2, group))
        for c in three:
            swaps += [exchange(c, 1, -1), exchange(c, 2, 1)]
        for copy in ends:
            copy.wait_recv()
        for c in three:
            swaps.append(exchange(c, 3, 2))
        for copy in swaps:
            copy.wait_recv()
        return started

    def rows_of(m):
        return pl.ds(pl.multiple_of(m * T, T), T)

    def product(k, m):
        return jnp.dot(fac[rows_of(m), k * NB:(k + 1) * NB], xs[k].reshape(NB, SCEN), preferred_element_type=jnp.float32)

    def first_product(m):
        total = None
        for half in range(2):
            right = xs[0, :, :, :, :, half].reshape(SCEN, 1024)
            left = fac[rows_of(m), half * 1024:(half + 1) * 1024]
            part = lax.dot_general(left, right, (((1,), (1,)), ((), ())), preferred_element_type=jnp.float32)
            total = part if total is None else total + part
        return total

    def turned(m):
        held = rt[:, :, :, :, :, rows_of(m)].reshape(SCEN, T)
        eye = (lax.broadcasted_iota(jnp.int32, (T, T), 0) == lax.broadcasted_iota(jnp.int32, (T, T), 1))
        return lax.dot_general(eye.astype(jnp.bfloat16), held, (((1,), (1,)), ((), ())), preferred_element_type=jnp.float32)

    def tiles(body):
        def one(m, carry):
            body(m)
            return carry
        lax.fori_loop(0, 4, one, 0)

    def multiply_first():
        def one(m):
            acc[rows_of(m), :] = first_product(m)
        tiles(one)

    def multiply(k):
        def one(m):
            kept = jnp.where(my_block == k, 0.0, acc[rows_of(m), :])
            acc[rows_of(m), :] = kept + product(k, m)
        tiles(one)

    def hand_out(k, m):
        parity = me % 2

        def send(dz, dx, target, place):
            pltpu.make_async_remote_copy(
                src_ref=staged.at[m, (at["z"] + dz) % 4, (at["x"] + dx) % 4], dst_ref=target, send_sem=sc_send,
                recv_sem=own_sem.at[k] if place is None else pass_recv.at[k, m],
                device_id=(m * 2 + parity, (at["z"] + dz) % 4 * 4 + (at["x"] + dx) % 4) if place is None
                else device(place, parity), device_id_type=MESH).start()

        most = max(len(RELAYS[way][m]) for way in WAYS)
        for i in range(most):
            for axis, by in WAYS:
                if i < len(RELAYS[axis, by][m]):
                    dz, dx = RELAYS[axis, by][m][i]
                    send(dz, dx, passing.at[k - 1, m, i], moved(axis, by))
        for dz in range(4):
            for dx in range(4):
                hops = sum(min(v, 4 - v) for v in (dz, dx, m))
                if hops > 1:
                    continue
                z, x = (at["z"] + dz) % 4, (at["x"] + dx) % 4
                target = xs.at[k, parity, m, z, x]
                if hops == 1:
                    send(dz, dx, target, None)
                else:
                    @pl.when(parity == 0)
                    def _():
                        pltpu.make_async_copy(staged.at[m, z, x], target, own_sem.at[k]).start()

                    @pl.when(parity == 1)
                    def _():
                        send(dz, dx, target, None)

    def solve(k, total, ready):
        for m in range(4):
            if ready:
                solved = turned(m) - total(m)
            else:
                solved = turned(m) - acc[rows_of(m), :]
            staged[m] = solved.astype(jnp.bfloat16).reshape(4, 4, 2, 8, SCEN)
            hand_out(k, m)

    def roles(k):
        dx = (at["x"] - (2 * k) % 4 - core) % 4
        dz = (at["z"] - k // 2) % 4
        offset = {"x": dx, "y": at["y"], "z": dz}
        for axis, by in WAYS:
            here = offset[axis] == by % 4
            for other in "xyz":
                if other != axis:
                    here = here & (offset[other] == 0)
            yield (axis, by), here

    def pass_on(k):
        for (axis, by), here in roles(k):
            @pl.when(here)
            def _():
                for m in range(4):
                    held = RELAYS[axis, by][m]
                    if not held:
                        continue
                    got = passing.at[k - 1, m, 0:len(held)]
                    pltpu.make_async_copy(got, got, pass_recv.at[k, m]).wait()
                    for i, (dz, dx) in enumerate(held):
                        z, x = (k // 2 + dz) % 4, ((2 * k) % 4 + core + dx) % 4
                        pltpu.make_async_remote_copy(
                            src_ref=passing.at[k - 1, m, i], dst_ref=xs.at[k, core, m, z, x], send_sem=pass_send.at[k],
                            recv_sem=own_sem.at[k], device_id=(m * 2 + core, z * 4 + x), device_id_type=MESH).start()

    def pass_done(k):
        for way, here in roles(k):
            @pl.when(here)
            def _():
                for m in range(4):
                    if RELAYS[way][m]:
                        got = passing.at[k - 1, m, 0:len(RELAYS[way][m])]
                        pltpu.make_async_copy(got, got, pass_send.at[k]).wait()

    loads = [load_factor(k) for k in range(STEPS)]
    for half in range(2):
        pltpu.make_async_copy(
            rhs.at[:, half * 1024:(half + 1) * 1024], xs.at[0, core, at["y"], at["z"], at["x"], half], own_sem.at[0]).start()
    mine = pltpu.make_async_copy(rows_to(me), rt.at[core, at["y"], at["z"], at["x"]], rt_recv)
    mine.start()

    for load in loads:
        load.start()

    barrier = pltpu.get_barrier_semaphore()
    for axis, by in WAYS:
        pl.semaphore_signal(barrier, inc=1, device_id=device(moved(axis, by), core), device_id_type=MESH)
    pl.semaphore_signal(barrier, inc=1, device_id=device(at, 1 - core), device_id_type=MESH)
    pl.semaphore_wait(barrier, 7)

    def own_piece(k):
        piece = xs.at[k, core, at["y"], at["z"], at["x"]]
        pltpu.make_async_copy(piece, piece, own_sem.at[k]).wait()

    own_piece(0)
    started = gather(0)
    for load in loads:
        load.wait()

    for owner in range(2, 8):
        @pl.when(me != owner)
        def _():
            rt_copy(jnp.int32(owner)).start()

    rt_batch(1, 36)

    @pl.when(my_block == 1)
    def _():
        multiply_first()
        rt_wait()
        solve(1, None, False)

    @pl.when(my_block != 1)
    def _():
        multiply_first()

    pass_on(1)
    own_piece(1)
    started += gather(1)
    for k in (2, 3):
        rt_batch(*{2: (36, 82), 3: (82, 128)}[k])

        @pl.when(my_block == k)
        def _():
            rt_wait()
            solve(k, lambda m: acc[rows_of(m), :] + product(k - 1, m), True)

        @pl.when(my_block != k)
        def _():
            multiply(k - 1)

        pass_on(k)
        own_piece(k)
        started += gather(k)

    is_owner = me < 2 * STEPS

    @pl.when((me < 2) | (me > 7))
    def _():
        rt_wait()

    def last(m):
        kept = jnp.where(my_block == STEPS - 1, 0.0, acc[rows_of(m), :])
        total = kept + product(STEPS - 1, m)
        value = jnp.where(is_owner, total, turned(m) - total)
        for c in range(2):
            for y in range(4):
                held = c * 4 + y
                out[rows_of(m), (y * 2 + c) * 128:(y * 2 + c + 1) * 128] = value[:, held * 128:(held + 1) * 128]
    tiles(last)

    for copy in started:
        copy.wait_send()
    pltpu.make_async_copy(rt.at[0], rt.at[0], rt_send).wait()
    pltpu.make_async_copy(rt.at[1, 0:3], rt.at[1, 0:3], rt_send).wait()
    pltpu.make_async_copy(rt.at[1, 3, 0:3], rt.at[1, 3, 0:3], rt_send).wait()
    pltpu.make_async_copy(rt.at[1, 3, 3, 0:3], rt.at[1, 3, 3, 0:3], rt_send).wait()

    @pl.when((me >= 2) & (me < 8))
    def _():
        @pl.when(me % 2 == 1)
        def _():
            pltpu.make_async_copy(staged, staged, sc_send).wait()

        @pl.when(me % 2 == 0)
        def _():
            pltpu.make_async_copy(staged.at[0:3], staged.at[0:3], sc_send).wait()
            pltpu.make_async_copy(staged.at[3, 0:3], staged.at[3, 0:3], sc_send).wait()
            pltpu.make_async_copy(staged.at[3, 3, 0:3], staged.at[3, 3, 0:3], sc_send).wait()


    for k in (1, 2, 3):
        pass_done(k)


def on_device(rhs_scen, factor_panels):
    dma = pltpu.SemaphoreType.DMA
    return pl.pallas_call(
        kernel,
        out_shape=pltpu.VMEM((ROWS, SCEN), jnp.float32),
        in_specs=[pl.BlockSpec(memory_space=pl.ANY)] * 2,
        out_specs=pl.BlockSpec(memory_space=pltpu.VMEM),
        scratch_shapes=[
            pltpu.VMEM((STEPS, 2, 4, 4, 4, 2, 8, 1024), jnp.bfloat16),
            pltpu.VMEM((ROWS, SCEN), jnp.float32),
            pltpu.VMEM((ROWS, STEPS * NB), jnp.bfloat16),
            pltpu.VMEM((2, 4, 4, 4, 8, ROWS), jnp.bfloat16),
            pltpu.VMEM((4, 4, 4, 2, 8, SCEN), jnp.bfloat16),
            pltpu.VMEM((STEPS - 1, 4, MOST, 2, 8, SCEN), jnp.bfloat16),
            dma((STEPS,)), dma((STEPS,)), dma((STEPS, 6, 3, 4)), dma((STEPS, 6, 3, 4)), dma((STEPS, 3, 4)), dma((STEPS, 3, 4)),
            dma, dma, dma, dma((STEPS, 4)), dma((STEPS,)),
        ],
        compiler_params=pltpu.CompilerParams(collective_id=0, has_side_effects=True, vmem_limit_bytes=52 * 1024 * 1024),
        name="substitute",
    )(rhs_scen, factor_panels)


def solution(mesh):
    placed = (P(("row", "col"), None), P(("row", "col"), None))
    return jax.shard_map(
        on_device, mesh=mesh, in_specs=placed, out_specs=P(("row", "col"), None), check_vma=False
    )
```

```python
import jax
import jax.numpy as jnp
from jax import lax
from jax.experimental import pallas as pl
from jax.experimental.pallas import tpu as pltpu
from jax.sharding import PartitionSpec as P

NB = 2048
STEPS = 4
ROWS = 1024
SCEN = 1024
T = 256
MESH = pl.DeviceIdType.MESH
ALL = slice(None)

COLOURS = (
    ("xzy", (0, ALL, pl.ds(0, 640)), (0, ALL, pl.ds(0, 384)), (0, ALL, pl.ds(384, 256))),
    ("yxz", (1, ALL, pl.ds(0, 640)), (1, ALL, pl.ds(0, 256)), (1, ALL, pl.ds(256, 384))),
    ("zyx", (ALL, ALL, pl.ds(640, 384)), (0, ALL, pl.ds(640, 384)), (1, ALL, pl.ds(640, 384))),
)
ORDER = (2, 1, 3, 0)
AXES = "yzx"

WAYS = [(axis, by) for axis in "xyz" for by in (1, -1)]


def plan_relays():
    relays = {way: [[] for _ in range(4)] for way in WAYS}
    load = dict.fromkeys(WAYS, 0)
    for far in (1, 2, 3):
        for m in range(4):
            for dz in range(4):
                for dx in range(4):
                    offset = {"x": dx, "y": m, "z": dz}
                    moving = [a for a in "xyz" if offset[a]]
                    hops = sum(min(v, 4 - v) for v in offset.values())
                    if len(moving) != far or hops == 1:
                        continue
                    ways = [w for w in WAYS if offset[w[0]] == 2 or offset[w[0]] == w[1] % 4]
                    way = min(ways, key=lambda w: (load[w] + len(relays[w][m]), WAYS.index(w)))
                    load[way] += 1
                    relays[way][m].append((dz, dx))
    return relays


RELAYS = plan_relays()
MOST = max(len(part) for parts in RELAYS.values() for part in parts)
TOTAL = max(sum(len(part) for part in parts) for parts in RELAYS.values())


def kernel(rhs, panels, out, xs, acc, fac, rt, staged, passing, feeding, own_sem, fac_sem, send_sem, near_sem, last_sem,
           far_sem, swap_sem, rt_send, rt_recv, sc_send, pass_recv, pass_send,
           feed_recv, feed_send):
    row, col = lax.axis_index("row"), lax.axis_index("col")
    me = row * 16 + col
    core = row % 2
    at = {"y": row // 2, "z": col // 4, "x": col % 4}
    my_block = me // 2

    def device(place, on_core):
        return (place["y"] * 2 + on_core, place["z"] * 4 + place["x"])

    def moved(axis, by):
        return {**at, axis: (at[axis] + by) % 4}

    def rows_to(dst):
        return rhs.at[:, pl.ds(pl.multiple_of(dst * ROWS, ROWS), ROWS)]

    def rt_copy(dst):
        return pltpu.make_async_remote_copy(
            src_ref=rows_to(dst), dst_ref=rt.at[core, at["y"], at["z"], at["x"]], send_sem=rt_send, recv_sem=rt_recv,
            device_id=(dst // 16, dst % 16), device_id_type=MESH)

    def rt_batch(first, last):
        def one(j, carry):
            dst = (me + j) % 128

            @pl.when((dst < 2) | (dst > 7))
            def _():
                rt_copy(dst).start()
            return carry
        lax.fori_loop(first, last, one, 0)

    def rt_wait():
        pltpu.make_async_copy(rt, rt, rt_recv).wait()

    def feeds():
        for h in range(2):
            dx = (at["x"] - 2 - h) % 4
            yield h, {"x": dx, "y": at["y"], "z": at["z"]}

    def away(offset):
        apart = [jnp.minimum(offset[a], 4 - offset[a]) for a in "xyz"]
        return apart[0] + apart[1] + apart[2]

    def listed(way):
        return [(dz, m, dx) for m in range(4) for dz, dx in RELAYS[way][m]]

    def feed():
        for h, offset in feeds():
            hops = away(offset)

            @pl.when((hops < 2) & (me != 2 + h))
            def _():
                rt_copy(jnp.int32(2 + h)).start()
            for way in WAYS:
                axis, by = way
                relay = {"x": 2 + h, "y": 0, "z": 0}
                relay[axis] = (relay[axis] + by) % 4
                for i, (dz, dy, dx) in enumerate(listed(way)):
                    @pl.when((offset["x"] == dx) & (offset["y"] == dy) & (offset["z"] == dz))
                    def _():
                        pltpu.make_async_remote_copy(
                            src_ref=rows_to(jnp.int32(2 + h)), dst_ref=feeding.at[i], send_sem=rt_send, recv_sem=feed_recv,
                            device_id=device(relay, core), device_id_type=MESH).start()

    def feed_roles():
        for h, offset in feeds():
            for axis, by in WAYS:
                here = offset[axis] == by % 4
                for other in "xyz":
                    if other != axis:
                        here = here & (offset[other] == 0)
                yield h, (axis, by), here

    def feed_on():
        for h, way, here in feed_roles():
            @pl.when(here)
            def _():
                held = listed(way)
                got = feeding.at[0:len(held)]
                pltpu.make_async_copy(got, got, feed_recv).wait()
                for i, (dz, dy, dx) in enumerate(held):
                    pltpu.make_async_remote_copy(
                        src_ref=feeding.at[i], dst_ref=rt.at[core, dy, dz, (2 + h + dx) % 4], send_sem=feed_send,
                        recv_sem=rt_recv, device_id=(0, 2 + h), device_id_type=MESH).start()

    def feed_done():
        for h, way, here in feed_roles():
            @pl.when(here)
            def _():
                got = feeding.at[0:len(listed(way))]
                pltpu.make_async_copy(got, got, feed_send).wait()

    def load_factor(k):
        cols = pl.ds(k * NB, NB)
        return pltpu.make_async_copy(panels.at[:, cols], fac.at[:, cols], fac_sem.at[k])

    def block_of(k, colour, fixed, part):
        return xs.at[(k, core) + tuple(fixed.get(a, ALL) for a in AXES) + part]

    def gather(k, between, first_half):
        turn = k % 2

        def send(block, sem, device_id):
            copy = pltpu.make_async_remote_copy(
                src_ref=block, dst_ref=block, send_sem=send_sem, recv_sem=sem, device_id=device_id, device_id_type=MESH)
            copy.start()
            return copy

        def ring(colour, phase, group, sem, by, centre, part):
            order = COLOURS[colour][0]
            axis, later = order[phase], order[phase + 1:]
            fixed = {a: at[a] for a in later}
            fixed[axis] = (at[axis] + centre) % 4
            if phase == 2:
                fixed[order[1]] = (at[order[1]] + group) % 4
            return send(block_of(k, colour, fixed, part), sem, device(moved(axis, by), core))

        def outward(colour, phase):
            whole = COLOURS[colour][1]
            return [ring(colour, phase, 0, near_sem.at[turn, phase, colour, lane], by, 0, whole)
                    for lane, by in enumerate((1, -1, 2))]

        def outward_last(colour, group):
            whole = COLOURS[colour][1]
            return [ring(colour, 2, group, last_sem.at[turn, group % 4, colour, lane], by, 0, whole)
                    for lane, by in enumerate((1, -1))]

        def forward(colour, group, copies):
            _, _, low, high = COLOURS[colour]
            copies[0].wait_recv()
            ring(colour, 2, group, far_sem.at[turn], 1, -1, low)
            copies[1].wait_recv()
            ring(colour, 2, group, far_sem.at[turn], -1, 1, high)

        def exchange(colour, centre):
            order, whole = COLOURS[colour][:2]
            axis = order[2]
            send(block_of(k, colour, {axis: (at[axis] + centre) % 4}, whole), swap_sem.at[turn], device(at, 1 - core))

        three = range(3)
        first = [outward(c, 0) for c in three]
        second = []
        for c in three:
            for copy in first[c]:
                copy.wait_recv()
            second.append(outward(c, 1))
        last = {(c, 0): outward_last(c, 0) for c in three}
        between[0]()
        for lane, group in enumerate((-1, 1, 2)):
            for c in three:
                second[c][lane].wait_recv()
                last[c, group] = outward_last(c, group)
        between[1]()
        for c in three:
            exchange(c, 0)
        for group in (0, -1, 1, 2):
            for c in three:
                forward(c, group, last[c, group])
        between[2]()
        for c in three:
            exchange(c, -1)
            exchange(c, 1)
        plane = xs.at[k, core, 0]
        other = xs.at[k, 1 - core]

        def own_half():
            pltpu.make_async_copy(plane, plane, far_sem.at[turn]).wait()
            for c in three:
                exchange(c, 2)

        def other_half():
            pltpu.make_async_copy(other, other, swap_sem.at[turn]).wait()

        @pl.when(core == 1)
        def _():
            own_half()

        @pl.when(core == 0)
        def _():
            other_half()
        first_half()

        @pl.when(core == 1)
        def _():
            other_half()

        @pl.when(core == 0)
        def _():
            own_half()

    def gathers_sent():
        for k in range(STEPS):
            for part in (xs.at[k, 0], xs.at[k, 1, 0:3], xs.at[k, 1, 3, 0:3], xs.at[k, 1, 3, 3, 0:3]):
                pltpu.make_async_copy(part, part, send_sem).wait()

    def rows_of(m):
        return pl.ds(pl.multiple_of(m * T, T), T)

    def product(k, half, m):
        cols = pl.ds(k * NB + half * 1024, 1024)
        return jnp.dot(fac[rows_of(m), cols], xs[k, half].reshape(1024, SCEN), preferred_element_type=jnp.float32)

    def first_product(half, m):
        total = None
        for part in range(2):
            right = xs[0, half, :, :, :, part].reshape(SCEN // 2, 1024)
            left = fac[rows_of(m), part * 1024:(part + 1) * 1024]
            more = lax.dot_general(left, right, (((1,), (1,)), ((), ())), preferred_element_type=jnp.float32)
            total = more if total is None else total + more
        return total

    def turned(m):
        held = rt[:, :, :, :, :, rows_of(m)].reshape(SCEN, T)
        eye = (lax.broadcasted_iota(jnp.int32, (T, T), 0) == lax.broadcasted_iota(jnp.int32, (T, T), 1))
        return lax.dot_general(eye.astype(jnp.bfloat16), held, (((1,), (1,)), ((), ())), preferred_element_type=jnp.float32)

    def tiles(body):
        def one(m, carry):
            body(m)
            return carry
        lax.fori_loop(0, 4, one, 0)

    def multiply(k, half):
        def one(m):
            if k == 0:
                acc[rows_of(m), half * 512:(half + 1) * 512] = first_product(half, m)
            elif half == 1:
                kept = jnp.where(my_block == k, 0.0, acc[rows_of(m), :])
                acc[rows_of(m), :] = kept + product(k, 1, m)
            else:
                acc[rows_of(m), :] += product(k, 0, m)
        tiles(one)

    def hand_out(k, m):
        parity = me % 2

        def send(dz, dx, target, place):
            pltpu.make_async_remote_copy(
                src_ref=staged.at[m, (at["z"] + dz) % 4, (at["x"] + dx) % 4], dst_ref=target, send_sem=sc_send,
                recv_sem=own_sem.at[k] if place is None else pass_recv.at[k - 1, m],
                device_id=(m * 2 + parity, (at["z"] + dz) % 4 * 4 + (at["x"] + dx) % 4) if place is None
                else device(place, parity), device_id_type=MESH).start()

        most = max(len(RELAYS[way][m]) for way in WAYS)
        for i in range(most):
            for axis, by in WAYS:
                if i < len(RELAYS[axis, by][m]):
                    dz, dx = RELAYS[axis, by][m][i]
                    send(dz, dx, passing.at[k - 1, m, i], moved(axis, by))
        for dz in range(4):
            for dx in range(4):
                hops = sum(min(v, 4 - v) for v in (dz, dx, m))
                if hops > 1:
                    continue
                z, x = (at["z"] + dz) % 4, (at["x"] + dx) % 4
                target = xs.at[k, parity, m, z, x]
                if hops == 1:
                    send(dz, dx, target, None)
                else:
                    @pl.when(parity == 0)
                    def _():
                        pltpu.make_async_copy(staged.at[m, z, x], target, own_sem.at[k]).start()

                    @pl.when(parity == 1)
                    def _():
                        send(dz, dx, target, None)

    def solve(k):
        for m in ORDER:
            wanted = turned(m)
            if k == 1:
                solved = wanted - jnp.concatenate([first_product(0, m), acc[rows_of(m), 512:]], axis=1)
            else:
                solved = wanted - (acc[rows_of(m), :] + product(k - 1, 0, m))
            staged[m] = solved.astype(jnp.bfloat16).reshape(4, 4, 2, 8, SCEN)
            hand_out(k, m)

    def roles(k):
        dx = (at["x"] - (2 * k) % 4 - core) % 4
        dz = (at["z"] - k // 2) % 4
        offset = {"x": dx, "y": at["y"], "z": dz}
        for axis, by in WAYS:
            here = offset[axis] == by % 4
            for other in "xyz":
                if other != axis:
                    here = here & (offset[other] == 0)
            yield (axis, by), here

    def pass_on(k):
        for (axis, by), here in roles(k):
            @pl.when(here)
            def _():
                for m in ORDER:
                    held = RELAYS[axis, by][m]
                    if not held:
                        continue
                    got = passing.at[k - 1, m, 0:len(held)]
                    pltpu.make_async_copy(got, got, pass_recv.at[k - 1, m]).wait()
                    for i, (dz, dx) in enumerate(held):
                        z, x = (k // 2 + dz) % 4, ((2 * k) % 4 + core + dx) % 4
                        pltpu.make_async_remote_copy(
                            src_ref=passing.at[k - 1, m, i], dst_ref=xs.at[k, core, m, z, x], send_sem=pass_send,
                            recv_sem=own_sem.at[k], device_id=(m * 2 + core, z * 4 + x), device_id_type=MESH).start()

    def pass_done(k):
        for way, here in roles(k):
            @pl.when(here)
            def _():
                for m in range(4):
                    if RELAYS[way][m]:
                        got = passing.at[k - 1, m, 0:len(RELAYS[way][m])]
                        pltpu.make_async_copy(got, got, pass_send).wait()

    loads = [load_factor(k) for k in range(STEPS)]
    for half in range(2):
        pltpu.make_async_copy(
            rhs.at[:, half * 1024:(half + 1) * 1024], xs.at[0, core, at["y"], at["z"], at["x"], half], own_sem.at[0]).start()
    mine = pltpu.make_async_copy(rows_to(me), rt.at[core, at["y"], at["z"], at["x"]], rt_recv)
    mine.start()

    for load in loads:
        load.start()

    barrier = pltpu.get_barrier_semaphore()
    for axis in AXES:
        for by in (1, 2, 3):
            pl.semaphore_signal(barrier, inc=1, device_id=device(moved(axis, by), core), device_id_type=MESH)
    pl.semaphore_signal(barrier, inc=1, device_id=device(at, 1 - core), device_id_type=MESH)

    expected = 10
    for h, offset in feeds():
        hops = away(offset)
        expected = expected + ((hops > 1) | ((hops == 1) & (core == 1))).astype(jnp.int32)

        @pl.when(me == 2 + h)
        def _():
            for axis, by in WAYS:
                pl.semaphore_signal(barrier, inc=1, device_id=device(moved(axis, by), 1), device_id_type=MESH)
    for h, way, here in feed_roles():
        @pl.when(here)
        def _():
            for dz, dy, dx in listed(way):
                place = {"y": dy, "z": dz, "x": (2 + h + dx) % 4}
                pl.semaphore_signal(barrier, inc=1, device_id=device(place, core), device_id_type=MESH)
    pl.semaphore_wait(barrier, expected)

    def own_piece(k):
        piece = xs.at[k, core, at["y"], at["z"], at["x"]]
        pltpu.make_async_copy(piece, piece, own_sem.at[k]).wait()

    def to_owners(*owners):
        for owner in owners:
            @pl.when(me != owner)
            def _():
                rt_copy(jnp.int32(owner)).start()

    def batch(first, last):
        return lambda: rt_batch(first, last)

    def nothing():
        pass

    own_piece(0)
    def load_wait():
        for load in loads:
            load.wait()

    def half_of(k):
        return lambda: multiply(k, 1)

    def first_half():
        load_wait()
        multiply(0, 1)

    slots = [(1, 1, 1, 13), (13, 19, 25, 55), (55, 59, 63, 91), (91, 99, 107, 128)]

    def after_first():
        to_owners(4, 5, 6, 7)
        rt_batch(slots[0][2], slots[0][3])

    gather(0, (feed, nothing, feed_on), first_half)
    after_first()
    for k in (1, 2, 3):
        @pl.when(my_block == k)
        def _():
            rt_wait()
            solve(k)

        @pl.when(my_block != k)
        def _():
            multiply(k - 1, 0)

        pass_on(k)
        own_piece(k)
        cuts = slots[k]
        gather(k, [batch(cuts[i], cuts[i + 1]) for i in range(3)], half_of(k))

    is_owner = me < 2 * STEPS

    @pl.when((me < 2) | (me > 7))
    def _():
        rt_wait()

    def last(m):
        total = acc[rows_of(m), :] + product(STEPS - 1, 0, m)
        value = jnp.where(is_owner, total, turned(m) - total)
        for c in range(2):
            for y in range(4):
                held = c * 4 + y
                out[rows_of(m), (y * 2 + c) * 128:(y * 2 + c + 1) * 128] = value[:, held * 128:(held + 1) * 128]
    tiles(last)

    gathers_sent()
    pltpu.make_async_copy(rt.at[0], rt.at[0], rt_send).wait()
    pltpu.make_async_copy(rt.at[1, 0:3], rt.at[1, 0:3], rt_send).wait()
    pltpu.make_async_copy(rt.at[1, 3, 0:3], rt.at[1, 3, 0:3], rt_send).wait()
    pltpu.make_async_copy(rt.at[1, 3, 3, 0:3], rt.at[1, 3, 3, 0:3], rt_send).wait()

    @pl.when((me >= 2) & (me < 8))
    def _():
        @pl.when(me % 2 == 1)
        def _():
            pltpu.make_async_copy(staged, staged, sc_send).wait()

        @pl.when(me % 2 == 0)
        def _():
            pltpu.make_async_copy(staged.at[0:3], staged.at[0:3], sc_send).wait()
            pltpu.make_async_copy(staged.at[3, 0:3], staged.at[3, 0:3], sc_send).wait()
            pltpu.make_async_copy(staged.at[3, 3, 0:3], staged.at[3, 3, 0:3], sc_send).wait()


    for k in (1, 2, 3):
        pass_done(k)
    feed_done()


def on_device(rhs_scen, factor_panels):
    dma = pltpu.SemaphoreType.DMA
    return pl.pallas_call(
        kernel,
        out_shape=pltpu.VMEM((ROWS, SCEN), jnp.float32),
        in_specs=[pl.BlockSpec(memory_space=pl.ANY)] * 2,
        out_specs=pl.BlockSpec(memory_space=pltpu.VMEM),
        scratch_shapes=[
            pltpu.VMEM((STEPS, 2, 4, 4, 4, 2, 8, 1024), jnp.bfloat16),
            pltpu.VMEM((ROWS, SCEN), jnp.float32),
            pltpu.VMEM((ROWS, STEPS * NB), jnp.bfloat16),
            pltpu.VMEM((2, 4, 4, 4, 8, ROWS), jnp.bfloat16),
            pltpu.VMEM((4, 4, 4, 2, 8, SCEN), jnp.bfloat16),
            pltpu.VMEM((STEPS - 1, 4, MOST, 2, 8, SCEN), jnp.bfloat16),
            pltpu.VMEM((TOTAL, 8, ROWS), jnp.bfloat16),
            dma((STEPS,)), dma((STEPS,)), dma, dma((2, 2, 3, 3)), dma((2, 4, 3, 2)), dma((2,)), dma((2,)),
            dma, dma, dma, dma((STEPS - 1, 4)), dma, dma, dma,
        ],
        compiler_params=pltpu.CompilerParams(collective_id=0, has_side_effects=True, vmem_limit_bytes=52 * 1024 * 1024),
        name="substitute",
    )(rhs_scen, factor_panels)


def solution(mesh):
    placed = (P(("row", "col"), None), P(("row", "col"), None))
    return jax.shard_map(
        on_device, mesh=mesh, in_specs=placed, out_specs=P(("row", "col"), None), check_vma=False
    )
```

```python
import jax
import jax.numpy as jnp
from jax import lax
from jax.experimental import pallas as pl
from jax.experimental.pallas import tpu as pltpu
from jax.sharding import PartitionSpec as P

NB = 2048
STEPS = 4
ROWS = 1024
SCEN = 1024
T = 256
MESH = pl.DeviceIdType.MESH
ALL = slice(None)

COLOURS = (
    ("xzy", (0, ALL, pl.ds(0, 640)), (0, ALL, pl.ds(0, 384)), (0, ALL, pl.ds(384, 256))),
    ("yxz", (1, ALL, pl.ds(0, 640)), (1, ALL, pl.ds(0, 256)), (1, ALL, pl.ds(256, 384))),
    ("zyx", (ALL, ALL, pl.ds(640, 384)), (0, ALL, pl.ds(640, 384)), (1, ALL, pl.ds(640, 384))),
)
ORDER = (2, 1, 3, 0)
AXES = "yzx"

WAYS = [(axis, by) for axis in "xyz" for by in (1, -1)]


def plan_relays():
    relays = {way: [[] for _ in range(4)] for way in WAYS}
    load = dict.fromkeys(WAYS, 0)
    for far in (1, 2, 3):
        for m in range(4):
            for dz in range(4):
                for dx in range(4):
                    offset = {"x": dx, "y": m, "z": dz}
                    moving = [a for a in "xyz" if offset[a]]
                    hops = sum(min(v, 4 - v) for v in offset.values())
                    if len(moving) != far or hops == 1:
                        continue
                    ways = [w for w in WAYS if offset[w[0]] == 2 or offset[w[0]] == w[1] % 4]
                    way = min(ways, key=lambda w: (load[w] + len(relays[w][m]), WAYS.index(w)))
                    load[way] += 1
                    relays[way][m].append((dz, dx))
    return relays


RELAYS = plan_relays()
MOST = max(len(part) for parts in RELAYS.values() for part in parts)
TOTAL = max(sum(len(part) for part in parts) for parts in RELAYS.values())


def kernel(rhs, panels, out, xs, acc, fac, rt, staged, passing, feeding, own_sem, fac_sem, send_sem, near_sem, last_sem,
           far_sem, swap_sem, rt_send, rt_recv, sc_send, pass_recv, pass_send,
           feed_recv, feed_send, known):
    row, col = lax.axis_index("row"), lax.axis_index("col")
    me = row * 16 + col
    core = row % 2
    at = {"y": row // 2, "z": col // 4, "x": col % 4}
    my_block = me // 2

    def device(place, on_core):
        return (place["y"] * 2 + on_core, place["z"] * 4 + place["x"])

    def moved(axis, by):
        return {**at, axis: (at[axis] + by) % 4}

    def rows_to(dst):
        return rhs.at[:, pl.ds(pl.multiple_of(dst * ROWS, ROWS), ROWS)]

    def rt_copy(dst):
        return pltpu.make_async_remote_copy(
            src_ref=rows_to(dst), dst_ref=rt.at[core, at["y"], at["z"], at["x"]], send_sem=rt_send, recv_sem=rt_recv,
            device_id=(dst // 16, dst % 16), device_id_type=MESH)

    def rt_batch(first, last):
        def one(j, carry):
            dst = (me + j) % 128

            @pl.when((dst < 2) | (dst > 7))
            def _():
                rt_copy(dst).start()
            return carry
        lax.fori_loop(first, last, one, 0)

    def rt_wait():
        pltpu.make_async_copy(rt, rt, rt_recv).wait()

    def feeds(b):
        for h in range(2):
            yield h, {"x": (at["x"] - 2 * b - h) % 4, "y": at["y"], "z": (at["z"] - b // 2) % 4}

    def away(offset):
        apart = [jnp.minimum(offset[a], 4 - offset[a]) for a in "xyz"]
        return apart[0] + apart[1] + apart[2]

    def listed(way):
        return [(dz, m, dx) for m in range(4) for dz, dx in RELAYS[way][m]]

    def feed(b):
        for h, offset in feeds(b):
            hops = away(offset)

            @pl.when((hops < 2) & (me != 2 * b + h))
            def _():
                rt_copy(jnp.int32(2 * b + h)).start()
            for way in WAYS:
                axis, by = way
                relay = {"x": (2 * b + h) % 4, "y": 0, "z": b // 2}
                relay[axis] = (relay[axis] + by) % 4
                for i, (dz, dy, dx) in enumerate(listed(way)):
                    @pl.when((offset["x"] == dx) & (offset["y"] == dy) & (offset["z"] == dz))
                    def _():
                        pltpu.make_async_remote_copy(
                            src_ref=rows_to(jnp.int32(2 * b + h)), dst_ref=feeding.at[b - 1, i], send_sem=rt_send,
                            recv_sem=feed_recv.at[b - 1],
                            device_id=device(relay, core), device_id_type=MESH).start()

    def feed_roles(b):
        for h, offset in feeds(b):
            for axis, by in WAYS:
                here = offset[axis] == by % 4
                for other in "xyz":
                    if other != axis:
                        here = here & (offset[other] == 0)
                yield h, (axis, by), here

    def feed_on(b):
        for h, way, here in feed_roles(b):
            @pl.when(here)
            def _():
                held = listed(way)
                got = feeding.at[b - 1, 0:len(held)]
                pltpu.make_async_copy(got, got, feed_recv.at[b - 1]).wait()
                for i, (dz, dy, dx) in enumerate(held):
                    pltpu.make_async_remote_copy(
                        src_ref=feeding.at[b - 1, i], dst_ref=rt.at[core, dy, (b // 2 + dz) % 4, (2 * b + h + dx) % 4],
                        send_sem=feed_send,
                        recv_sem=rt_recv, device_id=(0, 2 * b + h), device_id_type=MESH).start()

    def feed_done(b):
        for h, way, here in feed_roles(b):
            @pl.when(here)
            def _():
                got = feeding.at[b - 1, 0:len(listed(way))]
                pltpu.make_async_copy(got, got, feed_send).wait()

    def load_factor(k):
        cols = pl.ds(k * NB, NB)
        return pltpu.make_async_copy(panels.at[:, cols], fac.at[:, cols], fac_sem.at[k])

    def block_of(k, colour, fixed, part):
        return xs.at[(k, core) + tuple(fixed.get(a, ALL) for a in AXES) + part]

    def gather(k, between, first_half):
        turn = k % 2

        def send(block, sem, device_id):
            copy = pltpu.make_async_remote_copy(
                src_ref=block, dst_ref=block, send_sem=send_sem, recv_sem=sem, device_id=device_id, device_id_type=MESH)
            copy.start()
            return copy

        def ring(colour, phase, group, sem, by, centre, part):
            order = COLOURS[colour][0]
            axis, later = order[phase], order[phase + 1:]
            fixed = {a: at[a] for a in later}
            fixed[axis] = (at[axis] + centre) % 4
            if phase == 2:
                fixed[order[1]] = (at[order[1]] + group) % 4
            return send(block_of(k, colour, fixed, part), sem, device(moved(axis, by), core))

        def outward(colour, phase):
            whole = COLOURS[colour][1]
            return [ring(colour, phase, 0, near_sem.at[turn, phase, colour, lane], by, 0, whole)
                    for lane, by in enumerate((1, -1, 2))]

        def outward_last(colour, group):
            whole = COLOURS[colour][1]
            return [ring(colour, 2, group, last_sem.at[turn, group % 4, colour, lane], by, 0, whole)
                    for lane, by in enumerate((1, -1))]

        def forward(colour, group, copies):
            _, _, low, high = COLOURS[colour]
            copies[0].wait_recv()
            ring(colour, 2, group, far_sem.at[turn], 1, -1, low)
            copies[1].wait_recv()
            ring(colour, 2, group, far_sem.at[turn], -1, 1, high)

        def exchange(colour, centre):
            order, whole = COLOURS[colour][:2]
            axis = order[2]
            send(block_of(k, colour, {axis: (at[axis] + centre) % 4}, whole), swap_sem.at[turn], device(at, 1 - core))

        three = range(3)
        first = [outward(c, 0) for c in three]
        second = []
        for c in three:
            for copy in first[c]:
                copy.wait_recv()
            second.append(outward(c, 1))
        last = {(c, 0): outward_last(c, 0) for c in three}
        between[0]()
        for lane, group in enumerate((-1, 1, 2)):
            for c in three:
                second[c][lane].wait_recv()
                last[c, group] = outward_last(c, group)
        between[1]()
        for c in three:
            exchange(c, 0)
        for group in (0, -1, 1, 2):
            for c in three:
                forward(c, group, last[c, group])
        between[2]()
        for c in three:
            exchange(c, -1)
            exchange(c, 1)
        plane = xs.at[k, core, 0]
        other = xs.at[k, 1 - core]

        def own_half():
            pltpu.make_async_copy(plane, plane, far_sem.at[turn]).wait()
            for c in three:
                exchange(c, 2)

        def other_half():
            pltpu.make_async_copy(other, other, swap_sem.at[turn]).wait()

        @pl.when(core == 1)
        def _():
            own_half()

        @pl.when(core == 0)
        def _():
            other_half()
        first_half()

        @pl.when(core == 1)
        def _():
            other_half()

        @pl.when(core == 0)
        def _():
            own_half()

    def gathers_sent():
        for k in range(STEPS):
            for part in (xs.at[k, 0], xs.at[k, 1, 0:3], xs.at[k, 1, 3, 0:3], xs.at[k, 1, 3, 3, 0:3]):
                pltpu.make_async_copy(part, part, send_sem).wait()

    def rows_of(m):
        return pl.ds(pl.multiple_of(m * T, T), T)

    def product(k, half, m):
        cols = pl.ds(k * NB + half * 1024, 1024)
        return jnp.dot(fac[rows_of(m), cols], xs[k, half].reshape(1024, SCEN), preferred_element_type=jnp.float32)

    def first_product(half, m):
        total = None
        for part in range(2):
            right = xs[0, half, :, :, :, part].reshape(SCEN // 2, 1024)
            left = fac[rows_of(m), part * 1024:(part + 1) * 1024]
            more = lax.dot_general(left, right, (((1,), (1,)), ((), ())), preferred_element_type=jnp.float32)
            total = more if total is None else total + more
        return total

    def turned(m):
        held = rt[:, :, :, :, :, rows_of(m)].reshape(SCEN, T)
        eye = (lax.broadcasted_iota(jnp.int32, (T, T), 0) == lax.broadcasted_iota(jnp.int32, (T, T), 1))
        return lax.dot_general(eye.astype(jnp.bfloat16), held, (((1,), (1,)), ((), ())), preferred_element_type=jnp.float32)

    def tiles(body):
        def one(m, carry):
            body(m)
            return carry
        lax.fori_loop(0, 4, one, 0)

    def multiply(k, half):
        def one(m):
            if k == 0:
                acc[rows_of(m), half * 512:(half + 1) * 512] = first_product(half, m)
            elif half == 1:
                kept = jnp.where(my_block == k, 0.0, acc[rows_of(m), :])
                acc[rows_of(m), :] = kept + product(k, 1, m)
            else:
                acc[rows_of(m), :] += product(k, 0, m)
        tiles(one)

    def hand_out(k, m):
        parity = me % 2

        def send(dz, dx, target, place, way=None):
            pltpu.make_async_remote_copy(
                src_ref=staged.at[m, (at["z"] + dz) % 4, (at["x"] + dx) % 4], dst_ref=target, send_sem=sc_send,
                recv_sem=own_sem.at[k] if place is None else pass_recv.at[k - 1, m],
                device_id=(m * 2 + parity, (at["z"] + dz) % 4 * 4 + (at["x"] + dx) % 4) if place is None
                else device(place, 1 if way == WAYS[0] else parity), device_id_type=MESH).start()

        most = max(len(RELAYS[way][m]) for way in WAYS)
        for i in range(most):
            for axis, by in WAYS:
                if i < len(RELAYS[axis, by][m]):
                    dz, dx = RELAYS[axis, by][m][i]
                    send(dz, dx, passing.at[k - 1, m, i], moved(axis, by), (axis, by))
        for dz in range(4):
            for dx in range(4):
                hops = sum(min(v, 4 - v) for v in (dz, dx, m))
                if hops > 1:
                    continue
                z, x = (at["z"] + dz) % 4, (at["x"] + dx) % 4
                target = xs.at[k, parity, m, z, x]
                if hops == 1:
                    send(dz, dx, target, None)
                else:
                    @pl.when(parity == 0)
                    def _():
                        pltpu.make_async_copy(staged.at[m, z, x], target, own_sem.at[k]).start()

                    @pl.when(parity == 1)
                    def _():
                        send(dz, dx, target, None)

    def solve(k):
        for m in ORDER:
            wanted = turned(m)
            if k == 1:
                solved = wanted - jnp.concatenate([first_product(0, m), acc[rows_of(m), 512:]], axis=1)
            else:
                solved = wanted - (acc[rows_of(m), :] + product(k - 1, 0, m))
            staged[m] = solved.astype(jnp.bfloat16).reshape(4, 4, 2, 8, SCEN)
            hand_out(k, m)

    def roles(k):
        for way in WAYS:
            axis, by = way
            for h in (0, 1) if way == WAYS[0] else (core,):
                offset = {"x": (at["x"] - (2 * k) % 4 - h) % 4, "y": at["y"], "z": (at["z"] - k // 2) % 4}
                here = offset[axis] == by % 4
                for other in "xyz":
                    if other != axis:
                        here = here & (offset[other] == 0)
                yield way, h, here & (core == 1) if way == WAYS[0] else here

    def pass_on(k):
        for (axis, by), h, here in roles(k):
            @pl.when(here)
            def _():
                for m in ORDER:
                    held = RELAYS[axis, by][m]
                    if not held:
                        continue
                    got = passing.at[k - 1, m, 0:len(held)]
                    pltpu.make_async_copy(got, got, pass_recv.at[k - 1, m]).wait()
                    for i, (dz, dx) in enumerate(held):
                        z, x = (k // 2 + dz) % 4, ((2 * k) % 4 + h + dx) % 4
                        pltpu.make_async_remote_copy(
                            src_ref=passing.at[k - 1, m, i], dst_ref=xs.at[k, h, m, z, x], send_sem=pass_send,
                            recv_sem=own_sem.at[k], device_id=(m * 2 + h, z * 4 + x), device_id_type=MESH).start()

    def pass_done(k):
        for way, _, here in roles(k):
            @pl.when(here)
            def _():
                for m in range(4):
                    if RELAYS[way][m]:
                        got = passing.at[k - 1, m, 0:len(RELAYS[way][m])]
                        pltpu.make_async_copy(got, got, pass_send).wait()

    loads = [load_factor(k) for k in range(STEPS)]
    for half in range(2):
        pltpu.make_async_copy(
            rhs.at[:, half * 1024:(half + 1) * 1024], xs.at[0, core, at["y"], at["z"], at["x"], half], own_sem.at[0]).start()
    mine = pltpu.make_async_copy(rows_to(me), rt.at[core, at["y"], at["z"], at["x"]], rt_recv)
    mine.start()

    for load in loads:
        load.start()

    barrier = pltpu.get_barrier_semaphore()
    for axis in AXES:
        for by in (1, 2, 3):
            pl.semaphore_signal(barrier, inc=1, device_id=device(moved(axis, by), core), device_id_type=MESH)
    pl.semaphore_signal(barrier, inc=1, device_id=device(at, 1 - core), device_id_type=MESH)

    expected = 10
    for h, offset in feeds(1):
        hops = away(offset)
        expected = expected + ((hops > 1) | ((hops == 1) & (core == 1))).astype(jnp.int32)

        @pl.when(me == 2 + h)
        def _():
            for axis, by in WAYS:
                pl.semaphore_signal(barrier, inc=1, device_id=device(moved(axis, by), 1), device_id_type=MESH)
    for h, way, here in feed_roles(1):
        @pl.when(here)
        def _():
            for dz, dy, dx in listed(way):
                place = {"y": dy, "z": dz, "x": (2 + h + dx) % 4}
                pl.semaphore_signal(barrier, inc=1, device_id=device(place, core), device_id_type=MESH)
    pl.semaphore_wait(barrier, expected)

    def own_piece(k):
        piece = xs.at[k, core, at["y"], at["z"], at["x"]]
        pltpu.make_async_copy(piece, piece, own_sem.at[k]).wait()

    def batch(first, last):
        return lambda: rt_batch(first, last)

    def nothing():
        pass

    def load_wait():
        for load in loads:
            load.wait()

    def half_of(k):
        return lambda: multiply(k, 1)

    def first_half():
        load_wait()
        multiply(0, 1)

    slots = {0: (1, 1, 1, 27), 1: (27, 32, 37, 59), 2: (59, 64, 69, 91), 3: (91, 101, 111, 128)}

    for by in (1, 2, 3):
        pl.semaphore_signal(known.at[0], inc=1, device_id=device(moved("x", by), core), device_id_type=MESH)

    def opening():
        feed(1)
        pl.semaphore_wait(known.at[0], 3)
        for by in (1, 2, 3):
            pl.semaphore_signal(known.at[1], inc=1, device_id=device(moved("y", by), core), device_id_type=MESH)

    def all_known():
        pl.semaphore_wait(known.at[1], 3)
        pl.semaphore_signal(known.at[2], inc=1, device_id=device(at, 1 - core), device_id_type=MESH)
        pl.semaphore_wait(known.at[2], 1)
        feed(2)
        feed(3)
        rt_batch(slots[0][1], slots[0][2])

    def feeding_on():
        for b in (1, 2, 3):
            feed_on(b)
        rt_batch(slots[0][2], slots[0][3])

    own_piece(0)
    gather(0, (opening, all_known, feeding_on), first_half)
    for k in (1, 2, 3):
        @pl.when(my_block == k)
        def _():
            rt_wait()
            solve(k)

        @pl.when(my_block != k)
        def _():
            multiply(k - 1, 0)

        pass_on(k)
        own_piece(k)
        cuts = slots[k]

        def early():
            rt_batch(cuts[0], cuts[1])

        gather(k, (early, batch(cuts[1], cuts[2]), batch(cuts[2], cuts[3])), half_of(k))

    is_owner = me < 2 * STEPS

    @pl.when((me < 2) | (me > 7))
    def _():
        rt_wait()

    def last(m):
        total = acc[rows_of(m), :] + product(STEPS - 1, 0, m)
        value = jnp.where(is_owner, total, turned(m) - total)
        for c in range(2):
            for y in range(4):
                held = c * 4 + y
                out[rows_of(m), (y * 2 + c) * 128:(y * 2 + c + 1) * 128] = value[:, held * 128:(held + 1) * 128]
    tiles(last)

    gathers_sent()
    pltpu.make_async_copy(rt.at[0], rt.at[0], rt_send).wait()
    pltpu.make_async_copy(rt.at[1, 0:3], rt.at[1, 0:3], rt_send).wait()
    pltpu.make_async_copy(rt.at[1, 3, 0:3], rt.at[1, 3, 0:3], rt_send).wait()
    pltpu.make_async_copy(rt.at[1, 3, 3, 0:3], rt.at[1, 3, 3, 0:3], rt_send).wait()

    @pl.when((me >= 2) & (me < 8))
    def _():
        @pl.when(me % 2 == 1)
        def _():
            pltpu.make_async_copy(staged, staged, sc_send).wait()

        @pl.when(me % 2 == 0)
        def _():
            pltpu.make_async_copy(staged.at[0:3], staged.at[0:3], sc_send).wait()
            pltpu.make_async_copy(staged.at[3, 0:3], staged.at[3, 0:3], sc_send).wait()
            pltpu.make_async_copy(staged.at[3, 3, 0:3], staged.at[3, 3, 0:3], sc_send).wait()


    for k in (1, 2, 3):
        pass_done(k)
    for b in (1, 2, 3):
        feed_done(b)


def on_device(rhs_scen, factor_panels):
    dma = pltpu.SemaphoreType.DMA
    return pl.pallas_call(
        kernel,
        out_shape=pltpu.VMEM((ROWS, SCEN), jnp.float32),
        in_specs=[pl.BlockSpec(memory_space=pl.ANY)] * 2,
        out_specs=pl.BlockSpec(memory_space=pltpu.VMEM),
        scratch_shapes=[
            pltpu.VMEM((STEPS, 2, 4, 4, 4, 2, 8, 1024), jnp.bfloat16),
            pltpu.VMEM((ROWS, SCEN), jnp.float32),
            pltpu.VMEM((ROWS, STEPS * NB), jnp.bfloat16),
            pltpu.VMEM((2, 4, 4, 4, 8, ROWS), jnp.bfloat16),
            pltpu.VMEM((4, 4, 4, 2, 8, SCEN), jnp.bfloat16),
            pltpu.VMEM((STEPS - 1, 4, MOST, 2, 8, SCEN), jnp.bfloat16),
            pltpu.VMEM((STEPS - 1, TOTAL, 8, ROWS), jnp.bfloat16),
            dma((STEPS,)), dma((STEPS,)), dma, dma((2, 2, 3, 3)), dma((2, 4, 3, 2)), dma((2,)), dma((2,)),
            dma, dma, dma, dma((STEPS - 1, 4)), dma, dma((STEPS - 1,)), dma,
            pltpu.SemaphoreType.REGULAR((3,)),
        ],
        compiler_params=pltpu.CompilerParams(collective_id=0, has_side_effects=True, vmem_limit_bytes=52 * 1024 * 1024),
        name="substitute",
    )(rhs_scen, factor_panels)


def solution(mesh):
    placed = (P(("row", "col"), None), P(("row", "col"), None))
    return jax.shard_map(
        on_device, mesh=mesh, in_specs=placed, out_specs=P(("row", "col"), None), check_vma=False
    )
```

```python
import jax
import jax.numpy as jnp
from jax import lax
from jax.experimental import pallas as pl
from jax.experimental.pallas import tpu as pltpu
from jax.sharding import PartitionSpec as P

NB = 2048
STEPS = 4
ROWS = 1024
SCEN = 1024
T = 256
MESH = pl.DeviceIdType.MESH
ALL = slice(None)

COLOURS = (
    ("xzy", (0, ALL, pl.ds(0, 640)), (0, ALL, pl.ds(0, 384)), (0, ALL, pl.ds(384, 256))),
    ("yxz", (1, ALL, pl.ds(0, 640)), (1, ALL, pl.ds(0, 256)), (1, ALL, pl.ds(256, 384))),
    ("zyx", (ALL, ALL, pl.ds(640, 384)), (0, ALL, pl.ds(640, 384)), (1, ALL, pl.ds(640, 384))),
)
ORDER = (2, 1, 3, 0)
AXES = "yzx"

WAYS = [(axis, by) for axis in "xyz" for by in (1, -1)]


def plan_relays():
    relays = {way: [[] for _ in range(4)] for way in WAYS}
    load = dict.fromkeys(WAYS, 0)
    for far in (1, 2, 3):
        for m in range(4):
            for dz in range(4):
                for dx in range(4):
                    offset = {"x": dx, "y": m, "z": dz}
                    moving = [a for a in "xyz" if offset[a]]
                    hops = sum(min(v, 4 - v) for v in offset.values())
                    if len(moving) != far or hops == 1:
                        continue
                    ways = [w for w in WAYS if offset[w[0]] == 2 or offset[w[0]] == w[1] % 4]
                    way = min(ways, key=lambda w: (load[w] + len(relays[w][m]), WAYS.index(w)))
                    load[way] += 1
                    relays[way][m].append((dz, dx))
    return relays


RELAYS = plan_relays()
MOST = max(len(part) for parts in RELAYS.values() for part in parts)
TOTAL = max(sum(len(part) for part in parts) for parts in RELAYS.values())


def kernel(rhs, panels, out, xs, acc, fac, rt, staged, passing, feeding, own_sem, fac_sem, send_sem, near_sem, last_sem,
           far_sem, swap_sem, rt_send, rt_recv, sc_send, pass_recv, pass_send,
           feed_recv, feed_send, known):
    row, col = lax.axis_index("row"), lax.axis_index("col")
    me = row * 16 + col
    core = row % 2
    at = {"y": row // 2, "z": col // 4, "x": col % 4}
    my_block = me // 2

    def device(place, on_core):
        return (place["y"] * 2 + on_core, place["z"] * 4 + place["x"])

    def moved(axis, by):
        return {**at, axis: (at[axis] + by) % 4}

    def rows_to(dst):
        return rhs.at[:, pl.ds(pl.multiple_of(dst * ROWS, ROWS), ROWS)]

    def rt_copy(dst):
        return pltpu.make_async_remote_copy(
            src_ref=rows_to(dst), dst_ref=rt.at[core, at["y"], at["z"], at["x"]], send_sem=rt_send, recv_sem=rt_recv,
            device_id=(dst // 16, dst % 16), device_id_type=MESH)

    def rt_batch(first, last):
        def one(j, carry):
            dst = (me + j * 35) % 128

            @pl.when((dst < 2) | (dst > 7))
            def _():
                rt_copy(dst).start()
            return carry
        lax.fori_loop(first, last, one, 0)

    def rt_wait():
        pltpu.make_async_copy(rt, rt, rt_recv).wait()

    def feeds(b):
        for h in range(2):
            yield h, {"x": (at["x"] - 2 * b - h) % 4, "y": at["y"], "z": (at["z"] - b // 2) % 4}

    def away(offset):
        apart = [jnp.minimum(offset[a], 4 - offset[a]) for a in "xyz"]
        return apart[0] + apart[1] + apart[2]

    def listed(way):
        return [(dz, m, dx) for m in range(4) for dz, dx in RELAYS[way][m]]

    def feed(b):
        for h, offset in feeds(b):
            hops = away(offset)

            @pl.when((hops < 2) & (me != 2 * b + h))
            def _():
                rt_copy(jnp.int32(2 * b + h)).start()
            for way in WAYS:
                axis, by = way
                relay = {"x": (2 * b + h) % 4, "y": 0, "z": b // 2}
                relay[axis] = (relay[axis] + by) % 4
                for i, (dz, dy, dx) in enumerate(listed(way)):
                    @pl.when((offset["x"] == dx) & (offset["y"] == dy) & (offset["z"] == dz))
                    def _():
                        pltpu.make_async_remote_copy(
                            src_ref=rows_to(jnp.int32(2 * b + h)), dst_ref=feeding.at[b - 1, i], send_sem=rt_send,
                            recv_sem=feed_recv.at[b - 1],
                            device_id=device(relay, core), device_id_type=MESH).start()

    def feed_roles(b):
        for h, offset in feeds(b):
            for axis, by in WAYS:
                here = offset[axis] == by % 4
                for other in "xyz":
                    if other != axis:
                        here = here & (offset[other] == 0)
                yield h, (axis, by), here

    def feed_on(b):
        for h, way, here in feed_roles(b):
            @pl.when(here)
            def _():
                held = listed(way)
                got = feeding.at[b - 1, 0:len(held)]
                pltpu.make_async_copy(got, got, feed_recv.at[b - 1]).wait()
                for i, (dz, dy, dx) in enumerate(held):
                    pltpu.make_async_remote_copy(
                        src_ref=feeding.at[b - 1, i], dst_ref=rt.at[core, dy, (b // 2 + dz) % 4, (2 * b + h + dx) % 4],
                        send_sem=feed_send,
                        recv_sem=rt_recv, device_id=(0, 2 * b + h), device_id_type=MESH).start()

    def feed_done(b):
        for h, way, here in feed_roles(b):
            @pl.when(here)
            def _():
                got = feeding.at[b - 1, 0:len(listed(way))]
                pltpu.make_async_copy(got, got, feed_send).wait()

    def load_factor(k):
        cols = pl.ds(k * NB, NB)
        return pltpu.make_async_copy(panels.at[:, cols], fac.at[:, cols], fac_sem.at[k])

    def block_of(k, colour, fixed, part):
        return xs.at[(k, core) + tuple(fixed.get(a, ALL) for a in AXES) + part]

    def gather(k, between, first_half):
        turn = k % 2

        def send(block, sem, device_id):
            copy = pltpu.make_async_remote_copy(
                src_ref=block, dst_ref=block, send_sem=send_sem, recv_sem=sem, device_id=device_id, device_id_type=MESH)
            copy.start()
            return copy

        def ring(colour, phase, group, sem, by, centre, part):
            order = COLOURS[colour][0]
            axis, later = order[phase], order[phase + 1:]
            fixed = {a: at[a] for a in later}
            fixed[axis] = (at[axis] + centre) % 4
            if phase == 2:
                fixed[order[1]] = (at[order[1]] + group) % 4
            return send(block_of(k, colour, fixed, part), sem, device(moved(axis, by), core))

        def outward(colour, phase):
            whole = COLOURS[colour][1]
            return [ring(colour, phase, 0, near_sem.at[turn, phase, colour, lane], by, 0, whole)
                    for lane, by in enumerate((1, -1, 2))]

        def outward_last(colour, group):
            whole = COLOURS[colour][1]
            return [ring(colour, 2, group, last_sem.at[turn, group % 4, colour, lane], by, 0, whole)
                    for lane, by in enumerate((1, -1))]

        def forward(colour, group, copies):
            _, _, low, high = COLOURS[colour]
            copies[0].wait_recv()
            ring(colour, 2, group, far_sem.at[turn], 1, -1, low)
            copies[1].wait_recv()
            ring(colour, 2, group, far_sem.at[turn], -1, 1, high)

        def exchange(colour, centre):
            order, whole = COLOURS[colour][:2]
            axis = order[2]
            send(block_of(k, colour, {axis: (at[axis] + centre) % 4}, whole), swap_sem.at[turn], device(at, 1 - core))

        three = range(3)
        first = [outward(c, 0) for c in three]
        second = []
        for c in three:
            for copy in first[c]:
                copy.wait_recv()
            second.append(outward(c, 1))
        last = {(c, 0): outward_last(c, 0) for c in three}
        between[0]()
        for lane, group in enumerate((-1, 1, 2)):
            for c in three:
                second[c][lane].wait_recv()
                last[c, group] = outward_last(c, group)
        between[1]()
        for c in three:
            exchange(c, 0)
        for group in (0, -1, 1, 2):
            for c in three:
                forward(c, group, last[c, group])
        between[2]()
        for c in three:
            exchange(c, -1)
            exchange(c, 1)
        plane = xs.at[k, core, 0]
        other = xs.at[k, 1 - core]

        def own_half():
            pltpu.make_async_copy(plane, plane, far_sem.at[turn]).wait()
            for c in three:
                exchange(c, 2)

        def other_half():
            pltpu.make_async_copy(other, other, swap_sem.at[turn]).wait()

        @pl.when(core == 1)
        def _():
            own_half()

        @pl.when(core == 0)
        def _():
            other_half()
        first_half()

        @pl.when(core == 1)
        def _():
            other_half()

        @pl.when(core == 0)
        def _():
            own_half()

    def gathers_sent():
        for k in range(STEPS):
            for part in (xs.at[k, 0], xs.at[k, 1, 0:3], xs.at[k, 1, 3, 0:3], xs.at[k, 1, 3, 3, 0:3]):
                pltpu.make_async_copy(part, part, send_sem).wait()

    def rows_of(m):
        return pl.ds(pl.multiple_of(m * T, T), T)

    def product(k, half, m):
        cols = pl.ds(k * NB + half * 1024, 1024)
        return jnp.dot(fac[rows_of(m), cols], xs[k, half].reshape(1024, SCEN), preferred_element_type=jnp.float32)

    def first_product(half, m):
        total = None
        for part in range(2):
            right = xs[0, half, :, :, :, part].reshape(SCEN // 2, 1024)
            left = fac[rows_of(m), part * 1024:(part + 1) * 1024]
            more = lax.dot_general(left, right, (((1,), (1,)), ((), ())), preferred_element_type=jnp.float32)
            total = more if total is None else total + more
        return total

    def turned(m):
        held = rt[:, :, :, :, :, rows_of(m)].reshape(SCEN, T)
        eye = (lax.broadcasted_iota(jnp.int32, (T, T), 0) == lax.broadcasted_iota(jnp.int32, (T, T), 1))
        return lax.dot_general(eye.astype(jnp.bfloat16), held, (((1,), (1,)), ((), ())), preferred_element_type=jnp.float32)

    def tiles(body):
        def one(m, carry):
            body(m)
            return carry
        lax.fori_loop(0, 4, one, 0)

    def multiply(k, half):
        def one(m):
            if k == 0:
                acc[rows_of(m), half * 512:(half + 1) * 512] = first_product(half, m)
            elif half == 1:
                kept = jnp.where(my_block == k, 0.0, acc[rows_of(m), :])
                acc[rows_of(m), :] = kept + product(k, 1, m)
            else:
                acc[rows_of(m), :] += product(k, 0, m)
        tiles(one)

    def hand_out(k, m):
        parity = me % 2

        def send(dz, dx, target, place, way=None):
            pltpu.make_async_remote_copy(
                src_ref=staged.at[m, (at["z"] + dz) % 4, (at["x"] + dx) % 4], dst_ref=target, send_sem=sc_send,
                recv_sem=own_sem.at[k] if place is None else pass_recv.at[k - 1, m],
                device_id=(m * 2 + parity, (at["z"] + dz) % 4 * 4 + (at["x"] + dx) % 4) if place is None
                else device(place, 1 if way == WAYS[0] else parity), device_id_type=MESH).start()

        most = max(len(RELAYS[way][m]) for way in WAYS)
        for i in range(most):
            for axis, by in WAYS:
                if i < len(RELAYS[axis, by][m]):
                    dz, dx = RELAYS[axis, by][m][i]
                    send(dz, dx, passing.at[k - 1, m, i], moved(axis, by), (axis, by))
        for dz in range(4):
            for dx in range(4):
                hops = sum(min(v, 4 - v) for v in (dz, dx, m))
                if hops > 1:
                    continue
                z, x = (at["z"] + dz) % 4, (at["x"] + dx) % 4
                target = xs.at[k, parity, m, z, x]
                if hops == 1:
                    send(dz, dx, target, None)
                else:
                    @pl.when(parity == 0)
                    def _():
                        pltpu.make_async_copy(staged.at[m, z, x], target, own_sem.at[k]).start()

                    @pl.when(parity == 1)
                    def _():
                        send(dz, dx, target, None)

    def solve(k):
        for m in ORDER:
            wanted = turned(m)
            if k == 1:
                solved = wanted - jnp.concatenate([first_product(0, m), acc[rows_of(m), 512:]], axis=1)
            else:
                solved = wanted - (acc[rows_of(m), :] + product(k - 1, 0, m))
            staged[m] = solved.astype(jnp.bfloat16).reshape(4, 4, 2, 8, SCEN)
            hand_out(k, m)

    def roles(k):
        for way in WAYS:
            axis, by = way
            for h in (0, 1) if way == WAYS[0] else (core,):
                offset = {"x": (at["x"] - (2 * k) % 4 - h) % 4, "y": at["y"], "z": (at["z"] - k // 2) % 4}
                here = offset[axis] == by % 4
                for other in "xyz":
                    if other != axis:
                        here = here & (offset[other] == 0)
                yield way, h, here & (core == 1) if way == WAYS[0] else here

    def pass_on(k):
        for (axis, by), h, here in roles(k):
            @pl.when(here)
            def _():
                for m in ORDER:
                    held = RELAYS[axis, by][m]
                    if not held:
                        continue
                    got = passing.at[k - 1, m, 0:len(held)]
                    pltpu.make_async_copy(got, got, pass_recv.at[k - 1, m]).wait()
                    for i, (dz, dx) in enumerate(held):
                        z, x = (k // 2 + dz) % 4, ((2 * k) % 4 + h + dx) % 4
                        pltpu.make_async_remote_copy(
                            src_ref=passing.at[k - 1, m, i], dst_ref=xs.at[k, h, m, z, x], send_sem=pass_send,
                            recv_sem=own_sem.at[k], device_id=(m * 2 + h, z * 4 + x), device_id_type=MESH).start()

    def pass_done(k):
        for way, _, here in roles(k):
            @pl.when(here)
            def _():
                for m in range(4):
                    if RELAYS[way][m]:
                        got = passing.at[k - 1, m, 0:len(RELAYS[way][m])]
                        pltpu.make_async_copy(got, got, pass_send).wait()

    loads = [load_factor(k) for k in range(STEPS)]
    for half in range(2):
        pltpu.make_async_copy(
            rhs.at[:, half * 1024:(half + 1) * 1024], xs.at[0, core, at["y"], at["z"], at["x"], half], own_sem.at[0]).start()
    mine = pltpu.make_async_copy(rows_to(me), rt.at[core, at["y"], at["z"], at["x"]], rt_recv)
    mine.start()

    for load in loads:
        load.start()

    barrier = pltpu.get_barrier_semaphore()
    for axis in AXES:
        for by in (1, 2, 3):
            pl.semaphore_signal(barrier, inc=1, device_id=device(moved(axis, by), core), device_id_type=MESH)
    pl.semaphore_signal(barrier, inc=1, device_id=device(at, 1 - core), device_id_type=MESH)

    expected = 10
    for h, offset in feeds(1):
        hops = away(offset)
        expected = expected + ((hops > 1) | ((hops == 1) & (core == 1))).astype(jnp.int32)

        @pl.when(me == 2 + h)
        def _():
            for axis, by in WAYS:
                pl.semaphore_signal(barrier, inc=1, device_id=device(moved(axis, by), 1), device_id_type=MESH)
    for h, way, here in feed_roles(1):
        @pl.when(here)
        def _():
            for dz, dy, dx in listed(way):
                place = {"y": dy, "z": dz, "x": (2 + h + dx) % 4}
                pl.semaphore_signal(barrier, inc=1, device_id=device(place, core), device_id_type=MESH)
    pl.semaphore_wait(barrier, expected)

    def own_piece(k):
        piece = xs.at[k, core, at["y"], at["z"], at["x"]]
        pltpu.make_async_copy(piece, piece, own_sem.at[k]).wait()

    def batch(first, last):
        return lambda: rt_batch(first, last)

    def nothing():
        pass

    def load_wait():
        for load in loads:
            load.wait()

    def half_of(k):
        return lambda: multiply(k, 1)

    def first_half():
        load_wait()
        multiply(0, 1)

    slots = {0: (1, 1, 1, 31), 1: (31, 35, 39, 65), 2: (65, 69, 73, 99), 3: (99, 107, 115, 128)}

    for by in (1, 2, 3):
        pl.semaphore_signal(known.at[0], inc=1, device_id=device(moved("x", by), core), device_id_type=MESH)

    def opening():
        feed(1)
        pl.semaphore_wait(known.at[0], 3)
        for by in (1, 2, 3):
            pl.semaphore_signal(known.at[1], inc=1, device_id=device(moved("y", by), core), device_id_type=MESH)

    def all_known():
        pl.semaphore_wait(known.at[1], 3)
        pl.semaphore_signal(known.at[2], inc=1, device_id=device(at, 1 - core), device_id_type=MESH)
        pl.semaphore_wait(known.at[2], 1)
        feed(2)
        feed(3)
        rt_batch(slots[0][1], slots[0][2])

    def feeding_on():
        for b in (1, 2, 3):
            feed_on(b)
        rt_batch(slots[0][2], slots[0][3])

    own_piece(0)
    gather(0, (opening, all_known, feeding_on), first_half)
    for k in (1, 2, 3):
        @pl.when(my_block == k)
        def _():
            rt_wait()
            solve(k)

        @pl.when(my_block != k)
        def _():
            multiply(k - 1, 0)

        pass_on(k)
        own_piece(k)
        cuts = slots[k]

        def early():
            rt_batch(cuts[0], cuts[1])

        gather(k, (early, batch(cuts[1], cuts[2]), batch(cuts[2], cuts[3])), half_of(k))

    is_owner = me < 2 * STEPS

    @pl.when((me < 2) | (me > 7))
    def _():
        rt_wait()

    def last(m):
        total = acc[rows_of(m), :] + product(STEPS - 1, 0, m)
        value = jnp.where(is_owner, total, turned(m) - total)
        for c in range(2):
            for y in range(4):
                held = c * 4 + y
                out[rows_of(m), (y * 2 + c) * 128:(y * 2 + c + 1) * 128] = value[:, held * 128:(held + 1) * 128]
    tiles(last)

    gathers_sent()
    pltpu.make_async_copy(rt.at[0], rt.at[0], rt_send).wait()
    pltpu.make_async_copy(rt.at[1, 0:3], rt.at[1, 0:3], rt_send).wait()
    pltpu.make_async_copy(rt.at[1, 3, 0:3], rt.at[1, 3, 0:3], rt_send).wait()
    pltpu.make_async_copy(rt.at[1, 3, 3, 0:3], rt.at[1, 3, 3, 0:3], rt_send).wait()

    @pl.when((me >= 2) & (me < 8))
    def _():
        @pl.when(me % 2 == 1)
        def _():
            pltpu.make_async_copy(staged, staged, sc_send).wait()

        @pl.when(me % 2 == 0)
        def _():
            pltpu.make_async_copy(staged.at[0:3], staged.at[0:3], sc_send).wait()
            pltpu.make_async_copy(staged.at[3, 0:3], staged.at[3, 0:3], sc_send).wait()
            pltpu.make_async_copy(staged.at[3, 3, 0:3], staged.at[3, 3, 0:3], sc_send).wait()


    for k in (1, 2, 3):
        pass_done(k)
    for b in (1, 2, 3):
        feed_done(b)


def on_device(rhs_scen, factor_panels):
    dma = pltpu.SemaphoreType.DMA
    return pl.pallas_call(
        kernel,
        out_shape=pltpu.VMEM((ROWS, SCEN), jnp.float32),
        in_specs=[pl.BlockSpec(memory_space=pl.ANY)] * 2,
        out_specs=pl.BlockSpec(memory_space=pltpu.VMEM),
        scratch_shapes=[
            pltpu.VMEM((STEPS, 2, 4, 4, 4, 2, 8, 1024), jnp.bfloat16),
            pltpu.VMEM((ROWS, SCEN), jnp.float32),
            pltpu.VMEM((ROWS, STEPS * NB), jnp.bfloat16),
            pltpu.VMEM((2, 4, 4, 4, 8, ROWS), jnp.bfloat16),
            pltpu.VMEM((4, 4, 4, 2, 8, SCEN), jnp.bfloat16),
            pltpu.VMEM((STEPS - 1, 4, MOST, 2, 8, SCEN), jnp.bfloat16),
            pltpu.VMEM((STEPS - 1, TOTAL, 8, ROWS), jnp.bfloat16),
            dma((STEPS,)), dma((STEPS,)), dma, dma((2, 2, 3, 3)), dma((2, 4, 3, 2)), dma((2,)), dma((2,)),
            dma, dma, dma, dma((STEPS - 1, 4)), dma, dma((STEPS - 1,)), dma,
            pltpu.SemaphoreType.REGULAR((3,)),
        ],
        compiler_params=pltpu.CompilerParams(collective_id=0, has_side_effects=True, vmem_limit_bytes=52 * 1024 * 1024),
        name="substitute",
    )(rhs_scen, factor_panels)


def solution(mesh):
    placed = (P(("row", "col"), None), P(("row", "col"), None))
    return jax.shard_map(
        on_device, mesh=mesh, in_specs=placed, out_specs=P(("row", "col"), None), check_vma=False
    )
```
